128 devices in a mesh: gx: 16 (over x, y), gy: 8 (over z, core).
Axes of the slice: x: 4, y: 4, z: 4, core: 2. Of those that a mesh axis runs over, the one named last changes fastest.
Arguments:
- fine: bfloat16 [4096, 8, 256, 128], P(('gx', 'gy')), may hold values from -1500 to 1500
- patch_count: int32 [128], P(('gx', 'gy')), may hold values from 0 to 32, as said below
- block_place: int32 [128, 16], P(('gx', 'gy')), may hold values from 0 to 15, each once within a row
Outputs:
- factor: float32 [128, 128], replicated
- modes: bfloat16 [524288, 128], P(('gx', 'gy'))
The draws below stay inside these ranges and needn't reach their ends.
Inputs may be any that keep to these rules, and one draw needn't show every extreme that they name: `patch_count`: devices 2k and 2k + 1 in the numbering d = (index along gx) * 8 + (index along gy) hold 32 patches together; in every draw some even device holds 32 and some odd device holds 32.
All inputs are finite; a program needn't handle non-finite values.
Results may differ from the reference program's by a relative error of at most 0.004.
The reference program's roundings to bfloat16 on the way (of `coarse_slot` and `coarse`) count: a program that leaves them out, or rounds other values in their place, can miss the bound.
Values may be sent and summed in bfloat16 or wider, within the bound.
No kernel may reach another device: no remote copies, remote signals or barrier semaphores. Data moves between devices by JAX's collectives and lax.ppermute only.
A program may use at most 64 MiB of HBM per device.

```python
import math
import jax
import jax.numpy as jnp
from jax import lax

S = 128
PATCH = 256
CB = 16
PAIRS = 64
SLOTS_ALL = 4096
ROWS = 524288
N_GX = 16
N_GY = 8


def draw_fine(key, part):
    keys = jax.random.split(jax.random.fold_in(key, 11), 3)
    shape = (SLOTS_ALL, 8, PATCH, S)
    noise = jnp.clip(jax.random.normal(keys[0], shape, jnp.float32), -6.0, 6.0)
    column = jnp.exp(jax.random.uniform(keys[1], (S,), jnp.float32, 0.0, math.log(10.0)))
    cell = jnp.exp(jax.random.uniform(keys[2], (SLOTS_ALL, 1, PATCH, 1), jnp.float32, math.log(0.5), math.log(5.0)))
    device_pos = (jnp.arange(SLOTS_ALL) // (2 * CB)).astype(jnp.float32)
    device_scale = 1.0 + 2.0 * device_pos / (2 * PAIRS - 1)
    values = noise * column * cell * device_scale[:, None, None, None]
    return values.astype(jnp.bfloat16)


def draw_patch_count(key, part):
    keys = jax.random.split(jax.random.fold_in(key, 7), 3)
    excess = jax.random.randint(keys[0], (PAIRS,), -CB, CB + 1)
    first_pair = jax.random.randint(keys[1], (), 0, PAIRS)
    second_pair = (first_pair + 1 + jax.random.randint(keys[2], (), 0, PAIRS - 1)) % PAIRS
    excess = excess.at[first_pair].set(CB).at[second_pair].set(-CB)
    counts = jnp.stack([CB + excess, CB - excess], axis=1).reshape(2 * PAIRS)
    return counts.astype(jnp.int32)


def setup_inputs(seed: int = 0) -> dict:
    splits = jax.random.split(jax.random.key(seed), 4)
    return {
        "fine": draw_fine(jax.random.fold_in(splits[3], 71), 0),
        "patch_count": draw_patch_count(jax.random.fold_in(splits[3], 71), 0),
        "block_place": jax.vmap(lambda own: jax.random.permutation(own, CB))(jax.random.split(splits[2], (2 * PAIRS))).reshape((2 * PAIRS, CB)).astype(jnp.int32),
    }


def restrict_block(fine_block):
    return (lax.optimization_barrier(jnp.sum(fine_block, axis=1, dtype=jnp.float32)) * 0.125).astype(jnp.bfloat16)

def lower_factor(gram):
    width = gram.shape[0]
    index_col = jnp.arange(width, dtype=jnp.int32)

    def column_step(column, lower):
        partial_col = gram[:, column] - jnp.dot(lower, lower[column], precision=lax.Precision.HIGHEST)
        pivot = jnp.sqrt(partial_col[column])
        values = jnp.where(index_col > column, partial_col / pivot, jnp.where(index_col == column, pivot, 0.0))
        marker = (index_col == column).astype(jnp.float32)
        return lower + values[:, None] * marker[None, :]
    return lax.fori_loop(0, width, column_step, jnp.zeros((width, width), jnp.float32))

def lower_inverse(lower):
    width = lower.shape[0]
    index_col = jnp.arange(width, dtype=jnp.int32)
    identity = jnp.eye(width, dtype=jnp.float32)

    def row_step(row, inverse):
        known = jnp.where(index_col < row, lower[row], 0.0)
        values = (identity[row] - jnp.dot(known, inverse, precision=lax.Precision.HIGHEST)) / lower[row, row]
        marker = (index_col == row).astype(jnp.float32)
        return inverse + marker[:, None] * values[None, :]
    return lax.fori_loop(0, width, row_step, jnp.zeros((width, width), jnp.float32))

def reference(fine, patch_count, block_place):
    device_total = N_GX * N_GY
    slot_width = 2 * CB
    shaped = fine.reshape(device_total, slot_width, 8, PATCH, S)
    coarse_slot = lax.map(restrict_block, shaped).reshape(device_total * slot_width, PATCH, S)
    ends = jnp.cumsum(patch_count).astype(jnp.int32)
    starts = (ends - patch_count).astype(jnp.int32)
    block_ids = jnp.arange(device_total * CB, dtype=jnp.int32)
    holder = lax.optimization_barrier(jnp.sum((ends[None, :] <= block_ids[:, None]).astype(jnp.int32), axis=1)).astype(jnp.int32)
    source = (holder * slot_width + block_ids - starts[holder]).astype(jnp.int32)
    wanted = (jnp.arange(device_total, dtype=jnp.int32)[:, None] * CB + block_place).reshape(-1).astype(jnp.int32)
    coarse = jnp.take(coarse_slot, source[wanted], axis=0).reshape(ROWS, S)
    gram = lax.dot_general(coarse, coarse, (((0,), (0,)), ((), ())), preferred_element_type=jnp.float32) / ROWS
    lower = lower_factor(gram)
    factor = lower.T
    upper_inv = lower_inverse(lower).T
    modes = jnp.dot(coarse.astype(jnp.float32), upper_inv, precision=lax.Precision.HIGHEST)
    return (factor, modes.astype(jnp.bfloat16))
```

```python
import functools

import jax
import jax.numpy as jnp
from jax import lax
from jax.experimental import pallas as pl
from jax.experimental.pallas import tpu as pltpu
from jax.sharding import Mesh
from jax.sharding import PartitionSpec as P

ALL = ("x", "y", "z", "c")
TILE = 8


def parity_of():
    return lax.axis_index("c")


def front_kernel(scale, count_ref, fine_ref, avg_ref, out_ref, keep_ref, send_ref, buf, acc, sems):
    slots, children, cells, width = buf.shape
    half = slots // 2
    parity = parity_of()
    count = count_ref[0]

    def load(slot):
        return pltpu.make_async_copy(fine_ref.at[slot], buf.at[slot], sems.at[slot])

    def start(k, _):
        load(k).start()
        load(k + half).start()
        return 0

    lax.fori_loop(0, half, start, 0)
    acc[...] = jnp.zeros_like(acc)
    rows = 32

    def averaged(slot):
        for first in range(0, cells, rows):
            total = buf[slot, 0, first : first + rows, :].astype(jnp.float32)
            for child in range(1, children):
                total += buf[slot, child, first : first + rows, :].astype(jnp.float32)
            avg_ref[slot, first : first + rows, :] = (total * (1.0 / children)).astype(jnp.bfloat16)

    def cross(slot):
        value = avg_ref[slot]
        held = jnp.where(slot < count, value, jnp.zeros_like(value))
        return lax.dot_general(held, value, (((0,), (0,)), ((), ())), preferred_element_type=jnp.float32)

    def body(k, _):
        load(k).wait()
        averaged(k)
        load(k + half).wait()
        averaged(k + half)
        out_ref[k] = jnp.where(parity == 0, avg_ref[k + half], avg_ref[k])
        acc[...] += cross(k) + cross(k + half)
        return 0

    lax.fori_loop(0, half, body, 0)
    top = acc[: width // 2, :] * scale
    low = acc[width // 2 :, :] * scale
    keep_ref[...] = jnp.where(parity == 0, top, low)
    send_ref[...] = jnp.where(parity == 0, low, top)


def lane_spread(tile, lane):
    return jnp.broadcast_to(tile[:, lane : lane + 1], tile.shape)


def row_spread(tile, row):
    return jnp.broadcast_to(tile[row : row + 1, :], tile.shape)


def eliminate(rows):
    shape = rows[0].shape
    lane = lax.broadcasted_iota(jnp.int32, shape, 1)
    sub = lax.broadcasted_iota(jnp.int32, shape, 0)
    rows = list(rows)
    factor, inverse = [], []
    for t in range(len(rows)):
        base = t * TILE
        inside = (lane >= base) & (lane < base + TILE)
        panel = rows[t]
        columns = [lane_spread(panel, base + c) for c in range(TILE)]
        d = [[row_spread(columns[c], i) for c in range(i + 1)] for i in range(TILE)]
        upper = [row_spread(panel, i) for i in range(TILE)]
        mixed = [jnp.where(inside, (lane == base + i).astype(jnp.float32), upper[i]) for i in range(TILE)]
        inv = [None] * TILE
        for r in range(TILE):
            inv[r] = lax.rsqrt(d[r][r])
            for i in range(r + 1, TILE):
                d[i][r] = d[i][r] * inv[r]
            mixed[r] = mixed[r] * inv[r]
            upper[r] = upper[r] * inv[r]
            for i in range(r + 1, TILE):
                for c in range(r + 1, i + 1):
                    d[i][c] = d[i][c] - d[i][r] * d[c][r]
                mixed[i] = mixed[i] - d[i][r] * mixed[r]
                upper[i] = upper[i] - d[i][r] * upper[r]
        for j in range(t + 1, len(rows)):
            b = [lane_spread(rows[j], base + c) for c in range(TILE)]
            z = jnp.where(inside, 0.0, rows[j])
            for r in range(TILE):
                b[r] = b[r] * inv[r]
                for c in range(r + 1, TILE):
                    b[c] = b[c] - b[r] * d[c][r]
                z = z - b[r] * mixed[r]
            rows[j] = z
        f, m = jnp.zeros(shape, jnp.float32), jnp.zeros(shape, jnp.float32)
        for r in range(TILE):
            f = jnp.where((sub == r) & (lane >= base + r), upper[r], f)
            m = jnp.where((sub == r) & (lane <= base + r), mixed[r], m)
        factor.append(f)
        inverse.append(m)
    return factor, inverse


def back_kernel(
    count_ref, place_ref, mine_ref, other_ref, own_ref, moved_ref, factor_ref, modes_ref, gram, inv, buf, out, in_sems, out_sems
):
    blocks, cells, width = out.shape
    slots = buf.shape[0] - blocks
    parity = parity_of()
    count = count_ref[0]
    loads = (
        pltpu.make_async_copy(own_ref, buf.at[pl.ds(0, slots)], in_sems.at[0]),
        pltpu.make_async_copy(moved_ref, buf.at[pl.ds(slots, blocks)], in_sems.at[1]),
    )
    for load in loads:
        load.start()
    mine, other = mine_ref[...], other_ref[...]
    gram[: width // 2, :] = jnp.where(parity == 0, mine, other)
    gram[width // 2 :, :] = jnp.where(parity == 0, other, mine)
    factor, inverse = eliminate([gram[i : i + TILE, :] for i in range(0, width, TILE)])
    for t in range(width // TILE):
        factor_ref[t * TILE : (t + 1) * TILE, :] = factor[t]
        inv[t * TILE : (t + 1) * TILE, :] = inverse[t]
    for load in loads:
        load.wait()
    rest = inv[...]
    parts = []
    for _ in range(3):
        part = rest.astype(jnp.bfloat16)
        parts.append(part)
        rest = rest - part.astype(jnp.float32)

    def store(i):
        return pltpu.make_async_copy(out.at[i], modes_ref.at[pl.ds(i * cells, cells)], out_sems.at[i])

    for i in range(blocks):
        wanted = place_ref[i]
        excess = blocks - count
        from_even = jnp.where(wanted < count, wanted, slots + wanted - count)
        from_odd = jnp.where(wanted < excess, slots + wanted, wanted - excess)
        index = jnp.where(parity == 0, from_even, from_odd)
        value = buf[index]
        total = jnp.zeros((cells, width), jnp.float32)
        for part in reversed(parts):
            total += lax.dot_general(value, part, (((1,), (1,)), ((), ())), preferred_element_type=jnp.float32)
        out[i] = total.astype(jnp.bfloat16)
        store(i).start()
    for i in range(blocks):
        store(i).wait()


def spread_sum(value, axes, members):
    sent = jnp.broadcast_to(value[None], (members,) + value.shape)
    return jnp.sum(lax.all_to_all(sent, axes, 0, 0), axis=0)


def swapped(value):
    return lax.ppermute(value, "c", [(0, 1), (1, 0)])


def shards(fine, patch_count, block_place):
    slots, children, cells, width = fine.shape
    blocks = slots // 2
    devices = 1
    for axis in ALL:
        devices *= lax.axis_size(axis)
    row_total = blocks * cells * devices
    vmem, smem, hbm = pltpu.VMEM, pltpu.SMEM, pl.ANY
    spec = lambda space: pl.BlockSpec(memory_space=space)
    own, outgoing, keep, send = pl.pallas_call(
        functools.partial(front_kernel, 1.0 / row_total),
        out_shape=(
            jax.ShapeDtypeStruct((slots, cells, width), jnp.bfloat16),
            jax.ShapeDtypeStruct((blocks, cells, width), jnp.bfloat16),
            jax.ShapeDtypeStruct((width // 2, width), jnp.float32),
            jax.ShapeDtypeStruct((width // 2, width), jnp.float32),
        ),
        in_specs=[spec(smem), spec(hbm)],
        out_specs=[spec(vmem)] * 4,
        scratch_shapes=[
            pltpu.VMEM(fine.shape, jnp.bfloat16),
            pltpu.VMEM((width, width), jnp.float32),
            pltpu.SemaphoreType.DMA((slots,)),
        ],
        compiler_params=pltpu.CompilerParams(vmem_limit_bytes=50 * 2**20),
        name="front",
    )(patch_count, fine)
    half = keep + swapped(send)
    moved = swapped(outgoing)
    half = spread_sum(half, ("x", "y"), lax.axis_size("x") * lax.axis_size("y"))
    half = spread_sum(half, ("z",), lax.axis_size("z"))
    other = swapped(half)
    factor, modes = pl.pallas_call(
        back_kernel,
        out_shape=(
            jax.ShapeDtypeStruct((width, width), jnp.float32),
            jax.ShapeDtypeStruct((blocks * cells, width), jnp.bfloat16),
        ),
        in_specs=[spec(smem), spec(smem), spec(vmem), spec(vmem), spec(pl.ANY), spec(pl.ANY)],
        out_specs=[spec(vmem), spec(hbm)],
        scratch_shapes=[
            pltpu.VMEM((width, width), jnp.float32),
            pltpu.VMEM((width, width), jnp.float32),
            pltpu.VMEM((slots + blocks, cells, width), jnp.bfloat16),
            pltpu.VMEM((blocks, cells, width), jnp.bfloat16),
            pltpu.SemaphoreType.DMA((2,)),
            pltpu.SemaphoreType.DMA((blocks,)),
        ],
        compiler_params=pltpu.CompilerParams(vmem_limit_bytes=20 * 2**20),
        name="back",
    )(patch_count, block_place.reshape(-1), half, other, own, moved)
    return (factor, modes)


def solution(mesh):
    sizes = mesh.shape
    finer = Mesh(mesh.devices.reshape(4, sizes["gx"] // 4, sizes["gy"] // 2, 2), ALL)
    return jax.shard_map(
        shards,
        mesh=finer,
        in_specs=(P(ALL, None, None, None), P(ALL), P(ALL, None)),
        out_specs=(P(), P(ALL, None)),
        check_vma=False,
    )
```

```python
import functools

import jax
import jax.numpy as jnp
from jax import lax
from jax.experimental import pallas as pl
from jax.experimental.pallas import tpu as pltpu
from jax.sharding import Mesh
from jax.sharding import PartitionSpec as P

ALL = ("x", "y", "z", "c")
TILE = 8


def parity_of():
    return lax.axis_index("c")


def front_kernel(
    scale, groups, count_hbm, fine_ref, avg_ref, out_hbm, keep_ref, send_ref, buf, acc, count_ref, sems, out_sems, count_sem
):
    slots, children, cells, width = buf.shape
    half = slots // 2
    parity = parity_of()

    def load(slot):
        return pltpu.make_async_copy(fine_ref.at[slot], buf.at[slot], sems.at[slot])

    load_count = pltpu.make_async_copy(count_hbm, count_ref, count_sem.at[0])
    load_count.start()

    def sent_slot(k):
        return k + half * (1 - parity)

    def other_slot(k):
        return k + half * parity

    def start(k, _):
        load(sent_slot(k)).start()
        load(other_slot(k)).start()
        return 0

    lax.fori_loop(0, half, start, 0)
    load_count.wait()
    count = count_ref[0]
    rows = 32

    def send_out(k):
        return pltpu.make_async_copy(avg_ref.at[sent_slot(k)], out_hbm.at[k], out_sems.at[k])

    def averaged(slot):
        factor = jnp.where(slot < count, 1.0 / children, 0.0)
        for first in range(0, cells, rows):
            total = buf[slot, 0, first : first + rows, :].astype(jnp.float32)
            for child in range(1, children):
                total += buf[slot, child, first : first + rows, :].astype(jnp.float32)
            avg_ref[slot, first : first + rows, :] = (total * factor).astype(jnp.bfloat16)

    def body(k, _):
        load(sent_slot(k)).wait()
        averaged(sent_slot(k))
        send_out(k).start()
        load(other_slot(k)).wait()
        averaged(other_slot(k))
        return 0

    def cross(first, many):
        value = avg_ref[first : first + many].reshape(many * cells, width)
        return lax.dot_general(value, value, (((0,), (0,)), ((), ())), preferred_element_type=jnp.float32)

    done = 0
    for many in groups:
        lax.fori_loop(done, done + many, body, 0)
        part = cross(done, many) + cross(done + half, many)
        acc[...] = part if done == 0 else acc[...] + part
        done += many
    lane = lax.broadcasted_iota(jnp.int32, (width // 4, width), 1)
    strips = [acc[i : i + width // 4, :] * scale for i in range(0, width, width // 4)]
    second = jnp.where(lane < width // 4, pltpu.roll(strips[3], width // 4, 1), strips[1])
    cut = width // 8
    third = jnp.where(lane[:cut] < width // 2, pltpu.roll(strips[2][cut:], width // 2, 1), strips[2][:cut])
    packed = jnp.concatenate([strips[0], second, third], axis=0)
    middle = packed.shape[0] // 2
    top, low = packed[:middle], packed[middle:]
    keep_ref[...] = jnp.where(parity == 0, top, low)
    send_ref[...] = jnp.where(parity == 0, low, top)

    def finish(k, _):
        send_out(k).wait()
        return 0

    lax.fori_loop(0, half, finish, 0)


def unpacked(packed):
    width = packed.shape[1]
    quarter, cut = width // 4, width // 8
    second, third = packed[quarter : 2 * quarter], packed[2 * quarter :]
    upper = jnp.concatenate(
        [packed[: 2 * quarter], third, pltpu.roll(third, width // 2, 1), pltpu.roll(second, width - quarter, 1)], axis=0
    )
    row = lax.broadcasted_iota(jnp.int32, upper.shape, 0)
    lane = lax.broadcasted_iota(jnp.int32, upper.shape, 1)
    return jnp.where(lane // quarter >= row // quarter, upper, upper.T)


def lane_spread(tile, lane):
    return jnp.broadcast_to(tile[:, lane : lane + 1], tile.shape)


def row_spread(tile, row):
    return jnp.broadcast_to(tile[row : row + 1, :], tile.shape)


def eliminate(rows):
    shape = rows[0].shape
    lane = lax.broadcasted_iota(jnp.int32, shape, 1)
    sub = lax.broadcasted_iota(jnp.int32, shape, 0)
    rows = list(rows)
    factor, inverse = [], []
    for t in range(len(rows)):
        base = t * TILE
        inside = (lane >= base) & (lane < base + TILE)
        panel = rows[t]
        columns = [lane_spread(panel, base + c) for c in range(TILE)]
        d = [[row_spread(columns[c], i) for c in range(i + 1)] for i in range(TILE)]
        upper = [row_spread(panel, i) for i in range(TILE)]
        mixed = [jnp.where(inside, (lane == base + i).astype(jnp.float32), upper[i]) for i in range(TILE)]
        inv = [None] * TILE
        for r in range(TILE):
            inv[r] = lax.rsqrt(d[r][r])
            for i in range(r + 1, TILE):
                d[i][r] = d[i][r] * inv[r]
            mixed[r] = mixed[r] * inv[r]
            upper[r] = upper[r] * inv[r]
            for i in range(r + 1, TILE):
                for c in range(r + 1, i + 1):
                    d[i][c] = d[i][c] - d[i][r] * d[c][r]
                mixed[i] = mixed[i] - d[i][r] * mixed[r]
                upper[i] = upper[i] - d[i][r] * upper[r]
        for j in range(t + 1, len(rows)):
            b = [lane_spread(rows[j], base + c) for c in range(TILE)]
            z = jnp.where(inside, 0.0, rows[j])
            for r in range(TILE):
                b[r] = b[r] * inv[r]
                for c in range(r + 1, TILE):
                    b[c] = b[c] - b[r] * d[c][r]
                z = z - b[r] * mixed[r]
            rows[j] = z
        f, m = jnp.zeros(shape, jnp.float32), jnp.zeros(shape, jnp.float32)
        for r in range(TILE):
            f = jnp.where((sub == r) & (lane >= base + r), upper[r], f)
            m = jnp.where((sub == r) & (lane <= base + r), mixed[r], m)
        factor.append(f)
        inverse.append(m)
    return factor, inverse


def back_kernel(
    count_hbm, place_hbm, mine_ref, other_ref, own_ref, moved_ref, factor_ref, modes_ref, gram, inv, buf, out, count_ref, place_ref, in_sems, out_sems
):
    blocks, cells, width = out.shape
    slots = buf.shape[0] - blocks
    parity = parity_of()
    loads = (
        pltpu.make_async_copy(count_hbm, count_ref, in_sems.at[2]),
        pltpu.make_async_copy(place_hbm, place_ref, in_sems.at[3]),
        pltpu.make_async_copy(own_ref, buf.at[pl.ds(0, slots)], in_sems.at[0]),
        pltpu.make_async_copy(moved_ref, buf.at[pl.ds(slots, blocks)], in_sems.at[1]),
    )
    for load in loads:
        load.start()
    mine, other = mine_ref[...], other_ref[...]
    packed = jnp.concatenate([jnp.where(parity == 0, mine, other), jnp.where(parity == 0, other, mine)], axis=0)
    gram[...] = unpacked(packed)
    factor, inverse = eliminate([gram[i : i + TILE, :] for i in range(0, width, TILE)])
    for t in range(width // TILE):
        factor_ref[t * TILE : (t + 1) * TILE, :] = factor[t]
        inv[t * TILE : (t + 1) * TILE, :] = inverse[t]
    for load in loads:
        load.wait()
    count = count_ref[0]
    rest = inv[...]
    parts = []
    for _ in range(3):
        part = rest.astype(jnp.bfloat16)
        parts.append(part)
        rest = rest - part.astype(jnp.float32)

    def store(i):
        return pltpu.make_async_copy(out.at[i], modes_ref.at[pl.ds(i * cells, cells)], out_sems.at[i])

    for i in range(blocks):
        wanted = place_ref[0, i]
        excess = blocks - count
        from_even = jnp.where(wanted < count, wanted, slots + wanted - count)
        from_odd = jnp.where(wanted < excess, slots + wanted, wanted - excess)
        index = jnp.where(parity == 0, from_even, from_odd)
        value = buf[index]
        total = jnp.zeros((cells, width), jnp.float32)
        for part in reversed(parts):
            total += lax.dot_general(value, part, (((1,), (1,)), ((), ())), preferred_element_type=jnp.float32)
        out[i] = total.astype(jnp.bfloat16)
        store(i).start()
    for i in range(blocks):
        store(i).wait()


def spread_sum(value, axes, members):
    sent = jnp.broadcast_to(value[None], (members,) + value.shape)
    return jnp.sum(lax.all_to_all(sent, axes, 0, 0), axis=0)


def swapped(value):
    return lax.ppermute(value, "c", [(0, 1), (1, 0)])


def groups_of(total):
    return [total // 4] * 3 + [total // 4 - 1, 1]


def shards(fine, patch_count, block_place):
    slots, children, cells, width = fine.shape
    blocks = slots // 2
    devices = 1
    for axis in ALL:
        devices *= lax.axis_size(axis)
    row_total = blocks * cells * devices
    vmem, hbm = pltpu.VMEM, pl.ANY
    spec = lambda space: pl.BlockSpec(memory_space=space)
    own, outgoing, keep, send = pl.pallas_call(
        functools.partial(front_kernel, 1.0 / row_total, groups_of(blocks)),
        out_shape=(
            jax.ShapeDtypeStruct((slots, cells, width), jnp.bfloat16),
            jax.ShapeDtypeStruct((blocks, cells, width), jnp.bfloat16),
            jax.ShapeDtypeStruct((width * 5 // 16, width), jnp.float32),
            jax.ShapeDtypeStruct((width * 5 // 16, width), jnp.float32),
        ),
        in_specs=[spec(hbm), spec(hbm)],
        out_specs=[spec(vmem), spec(hbm), spec(vmem), spec(vmem)],
        scratch_shapes=[
            pltpu.VMEM(fine.shape, jnp.bfloat16),
            pltpu.VMEM((width, width), jnp.float32),
            pltpu.SMEM((1,), jnp.int32),
            pltpu.SemaphoreType.DMA((slots,)),
            pltpu.SemaphoreType.DMA((blocks,)),
            pltpu.SemaphoreType.DMA((1,)),
        ],
        compiler_params=pltpu.CompilerParams(vmem_limit_bytes=50 * 2**20),
        name="front",
    )(patch_count, fine)
    half = keep + swapped(send)
    half, outgoing = lax.optimization_barrier((half, outgoing))
    moved = swapped(outgoing)
    half = spread_sum(half, ("x", "y"), lax.axis_size("x") * lax.axis_size("y"))
    half = spread_sum(half, ("z",), lax.axis_size("z"))
    other = swapped(half)
    factor, modes = pl.pallas_call(
        back_kernel,
        out_shape=(
            jax.ShapeDtypeStruct((width, width), jnp.float32),
            jax.ShapeDtypeStruct((blocks * cells, width), jnp.bfloat16),
        ),
        in_specs=[spec(hbm), spec(hbm), spec(vmem), spec(vmem), spec(hbm), spec(hbm)],
        out_specs=[spec(vmem), spec(hbm)],
        scratch_shapes=[
            pltpu.VMEM((width, width), jnp.float32),
            pltpu.VMEM((width, width), jnp.float32),
            pltpu.VMEM((slots + blocks, cells, width), jnp.bfloat16),
            pltpu.VMEM((blocks, cells, width), jnp.bfloat16),
            pltpu.SMEM((1,), jnp.int32),
            pltpu.SMEM((1, blocks), jnp.int32),
            pltpu.SemaphoreType.DMA((4,)),
            pltpu.SemaphoreType.DMA((blocks,)),
        ],
        compiler_params=pltpu.CompilerParams(vmem_limit_bytes=20 * 2**20),
        name="back",
    )(patch_count, block_place, half, other, own, moved)
    return (factor, modes)


def solution(mesh):
    sizes = mesh.shape
    finer = Mesh(mesh.devices.reshape(4, sizes["gx"] // 4, sizes["gy"] // 2, 2), ALL)
    return jax.shard_map(
        shards,
        mesh=finer,
        in_specs=(P(ALL, None, None, None), P(ALL), P(ALL, None)),
        out_specs=(P(), P(ALL, None)),
        check_vma=False,
    )
```

```python
import functools

import jax
import jax.numpy as jnp
from jax import lax
from jax.experimental import pallas as pl
from jax.experimental.pallas import tpu as pltpu
from jax.sharding import Mesh
from jax.sharding import PartitionSpec as P

ALL = ("x", "y", "z", "c")
TILE = 8


def parity_of():
    return lax.axis_index("c")


def front_kernel(
    scale, groups, count_hbm, fine_ref, avg_ref, out_hbm, part_ref, buf, acc, count_ref, sems, out_sems, count_sem
):
    slots, children, cells, width = buf.shape
    half = slots // 2
    parity = parity_of()

    def load(slot):
        return pltpu.make_async_copy(fine_ref.at[slot], buf.at[slot], sems.at[slot])

    load_count = pltpu.make_async_copy(count_hbm, count_ref, count_sem.at[0])
    load_count.start()

    first_sent = half * (1 - parity)
    first_kept = half * parity

    def start(k, _, first):
        load(first + k).start()
        return 0

    for first in (first_sent, first_kept):
        lax.fori_loop(0, half, functools.partial(start, first=first), 0)
    load_count.wait()
    count = count_ref[0]
    rows = 32

    def send_out(k):
        return pltpu.make_async_copy(avg_ref.at[first_sent + k], out_hbm.at[k], out_sems.at[k])

    def averaged(slot):
        factor = jnp.where(slot < count, 1.0 / children, 0.0)
        for first in range(0, cells, rows):
            total = buf[slot, 0, first : first + rows, :].astype(jnp.float32)
            for child in range(1, children):
                total += buf[slot, child, first : first + rows, :].astype(jnp.float32)
            avg_ref[slot, first : first + rows, :] = (total * factor).astype(jnp.bfloat16)

    def body(k, _, first):
        load(first + k).wait()
        averaged(first + k)
        if first is first_sent:
            send_out(k).start()
        return 0

    def cross(slot, many):
        value = avg_ref[pl.ds(slot, many)].reshape(many * cells, width)
        return lax.dot_general(value, value, (((0,), (0,)), ((), ())), preferred_element_type=jnp.float32)

    acc[...] = jnp.zeros_like(acc)
    for first, runs in zip((first_sent, first_kept), groups):
        done = 0
        for many in runs:
            lax.fori_loop(done, done + many, functools.partial(body, first=first), 0)
            acc[...] += cross(first + done, many)
            done += many
    lane = lax.broadcasted_iota(jnp.int32, (width // 4, width), 1)
    strips = [acc[i : i + width // 4, :] * scale for i in range(0, width, width // 4)]
    second = jnp.where(lane < width // 4, pltpu.roll(strips[3], width // 4, 1), strips[1])
    cut = width // 8
    third = jnp.where(lane[:cut] < width // 2, pltpu.roll(strips[2][cut:], width // 2, 1), strips[2][:cut])
    packed = jnp.concatenate([strips[0], second, third], axis=0)
    members, cores, middle, _ = part_ref.shape
    for core in range(cores):
        for member in range(members):
            part_ref[member, core] = packed[core * middle : (core + 1) * middle]

    def finish(k, _):
        send_out(k).wait()
        return 0

    lax.fori_loop(0, half, finish, 0)


def unpacked(packed):
    width = packed.shape[1]
    quarter, cut = width // 4, width // 8
    second, third = packed[quarter : 2 * quarter], packed[2 * quarter :]
    upper = jnp.concatenate(
        [packed[: 2 * quarter], third, pltpu.roll(third, width // 2, 1), pltpu.roll(second, width - quarter, 1)], axis=0
    )
    row = lax.broadcasted_iota(jnp.int32, upper.shape, 0)
    lane = lax.broadcasted_iota(jnp.int32, upper.shape, 1)
    return jnp.where(lane // quarter >= row // quarter, upper, upper.T)


def lane_spread(tile, lane):
    return jnp.broadcast_to(tile[:, lane : lane + 1], tile.shape)


def row_spread(tile, row):
    return jnp.broadcast_to(tile[row : row + 1, :], tile.shape)


def eliminate(rows):
    shape = rows[0].shape
    lane = lax.broadcasted_iota(jnp.int32, shape, 1)
    sub = lax.broadcasted_iota(jnp.int32, shape, 0)
    rows = list(rows)
    factor, inverse = [], []
    for t in range(len(rows)):
        base = t * TILE
        inside = (lane >= base) & (lane < base + TILE)
        panel = rows[t]
        columns = [lane_spread(panel, base + c) for c in range(TILE)]
        d = [[row_spread(columns[c], i) for c in range(i + 1)] for i in range(TILE)]
        upper = [row_spread(panel, i) for i in range(TILE)]
        mixed = [jnp.where(inside, (lane == base + i).astype(jnp.float32), upper[i]) for i in range(TILE)]
        inv = [None] * TILE
        for r in range(TILE):
            inv[r] = lax.rsqrt(d[r][r])
            for i in range(r + 1, TILE):
                d[i][r] = d[i][r] * inv[r]
            mixed[r] = mixed[r] * inv[r]
            upper[r] = upper[r] * inv[r]
            for i in range(r + 1, TILE):
                for c in range(r + 1, i + 1):
                    d[i][c] = d[i][c] - d[i][r] * d[c][r]
                mixed[i] = mixed[i] - d[i][r] * mixed[r]
                upper[i] = upper[i] - d[i][r] * upper[r]
        for j in range(t + 1, len(rows)):
            b = [lane_spread(rows[j], base + c) for c in range(TILE)]
            z = jnp.where(inside, 0.0, rows[j])
            for r in range(TILE):
                b[r] = b[r] * inv[r]
                for c in range(r + 1, TILE):
                    b[c] = b[c] - b[r] * d[c][r]
                z = z - b[r] * mixed[r]
            rows[j] = z
        f, m = jnp.zeros(shape, jnp.float32), jnp.zeros(shape, jnp.float32)
        for r in range(TILE):
            f = jnp.where((sub == r) & (lane >= base + r), upper[r], f)
            m = jnp.where((sub == r) & (lane <= base + r), mixed[r], m)
        factor.append(f)
        inverse.append(m)
    return factor, inverse


def back_kernel(
    count_hbm, place_hbm, mine_ref, other_ref, own_ref, moved_ref, factor_ref, modes_ref, gram, inv, buf, out, count_ref, place_ref, in_sems, out_sems
):
    blocks, cells, width = out.shape
    slots = buf.shape[0] - blocks
    parity = parity_of()
    loads = (
        pltpu.make_async_copy(count_hbm, count_ref, in_sems.at[2]),
        pltpu.make_async_copy(place_hbm, place_ref, in_sems.at[3]),
        pltpu.make_async_copy(own_ref, buf.at[pl.ds(0, slots)], in_sems.at[0]),
        pltpu.make_async_copy(moved_ref, buf.at[pl.ds(slots, blocks)], in_sems.at[1]),
    )
    for load in loads:
        load.start()
    mine, other = mine_ref[...], other_ref[...]
    packed = jnp.concatenate([jnp.where(parity == 0, mine, other), jnp.where(parity == 0, other, mine)], axis=0)
    gram[...] = unpacked(packed)
    factor, inverse = eliminate([gram[i : i + TILE, :] for i in range(0, width, TILE)])
    for t in range(width // TILE):
        factor_ref[t * TILE : (t + 1) * TILE, :] = factor[t]
        inv[t * TILE : (t + 1) * TILE, :] = inverse[t]
    for load in loads:
        load.wait()
    count = count_ref[0]
    rest = inv[...]
    parts = []
    for _ in range(3):
        part = rest.astype(jnp.bfloat16)
        parts.append(part)
        rest = rest - part.astype(jnp.float32)
    terms = jnp.concatenate(parts, axis=1)

    def store(i):
        return pltpu.make_async_copy(out.at[i], modes_ref.at[pl.ds(i * cells, cells)], out_sems.at[i])

    for i in range(blocks):
        wanted = place_ref[0, i]
        excess = blocks - count
        from_even = jnp.where(wanted < count, wanted, slots + wanted - count)
        from_odd = jnp.where(wanted < excess, slots + wanted, wanted - excess)
        index = jnp.where(parity == 0, from_even, from_odd)
        value = buf[index]
        repeated = jnp.concatenate([value] * len(parts), axis=1)
        total = lax.dot_general(repeated, terms, (((1,), (1,)), ((), ())), preferred_element_type=jnp.float32)
        out[i] = total.astype(jnp.bfloat16)
        store(i).start()
    for i in range(blocks):
        store(i).wait()


def swapped(value):
    return lax.ppermute(value, "c", [(0, 1), (1, 0)])


def groups_of(total):
    return [total], [total // 2, total // 2 - 2, 2]


def shards(fine, patch_count, block_place):
    slots, children, cells, width = fine.shape
    blocks = slots // 2
    devices = 1
    for axis in ALL:
        devices *= lax.axis_size(axis)
    row_total = blocks * cells * devices
    vmem, hbm = pltpu.VMEM, pl.ANY
    spec = lambda space: pl.BlockSpec(memory_space=space)
    own, outgoing, parts = pl.pallas_call(
        functools.partial(front_kernel, 1.0 / row_total, groups_of(blocks)),
        out_shape=(
            jax.ShapeDtypeStruct((slots, cells, width), jnp.bfloat16),
            jax.ShapeDtypeStruct((blocks, cells, width), jnp.bfloat16),
            jax.ShapeDtypeStruct((lax.axis_size("z"), 2, width * 5 // 16, width), jnp.float32),
        ),
        in_specs=[spec(hbm), spec(hbm)],
        out_specs=[spec(vmem), spec(pltpu.HBM), spec(vmem)],
        scratch_shapes=[
            pltpu.VMEM(fine.shape, jnp.bfloat16),
            pltpu.VMEM((width, width), jnp.float32),
            pltpu.SMEM((1,), jnp.int32),
            pltpu.SemaphoreType.DMA((slots,)),
            pltpu.SemaphoreType.DMA((blocks,)),
            pltpu.SemaphoreType.DMA((1,)),
        ],
        compiler_params=pltpu.CompilerParams(vmem_limit_bytes=50 * 2**20),
        name="front",
    )(patch_count, fine)
    parts = parts.reshape((-1,) + parts.shape[2:])
    half = jnp.sum(lax.all_to_all(parts, ("z", "c"), 0, 0), axis=0)

    moved = swapped(outgoing)
    sent = jnp.broadcast_to(half[None], (lax.axis_size("x") * lax.axis_size("y"),) + half.shape)
    half = jnp.sum(lax.all_to_all(sent, ("x", "y"), 0, 0), axis=0)
    other = swapped(half)
    factor, modes = pl.pallas_call(
        back_kernel,
        out_shape=(
            jax.ShapeDtypeStruct((width, width), jnp.float32),
            jax.ShapeDtypeStruct((blocks * cells, width), jnp.bfloat16),
        ),
        in_specs=[spec(hbm), spec(hbm), spec(vmem), spec(vmem), spec(hbm), spec(hbm)],
        out_specs=[spec(vmem), spec(hbm)],
        scratch_shapes=[
            pltpu.VMEM((width, width), jnp.float32),
            pltpu.VMEM((width, width), jnp.float32),
            pltpu.VMEM((slots + blocks, cells, width), jnp.bfloat16),
            pltpu.VMEM((blocks, cells, width), jnp.bfloat16),
            pltpu.SMEM((1,), jnp.int32),
            pltpu.SMEM((1, blocks), jnp.int32),
            pltpu.SemaphoreType.DMA((4,)),
            pltpu.SemaphoreType.DMA((blocks,)),
        ],
        compiler_params=pltpu.CompilerParams(vmem_limit_bytes=20 * 2**20),
        name="back",
    )(patch_count, block_place, half, other, own, moved)
    return (factor, modes)


def solution(mesh):
    sizes = mesh.shape
    finer = Mesh(mesh.devices.reshape(4, sizes["gx"] // 4, sizes["gy"] // 2, 2), ALL)
    return jax.shard_map(
        shards,
        mesh=finer,
        in_specs=(P(ALL, None, None, None), P(ALL), P(ALL, None)),
        out_specs=(P(), P(ALL, None)),
        check_vma=False,
    )
```

```python
import functools

import jax
import jax.numpy as jnp
from jax import lax
from jax.experimental import pallas as pl
from jax.experimental.pallas import tpu as pltpu
from jax.sharding import Mesh
from jax.sharding import PartitionSpec as P

ALL = ("x", "y", "z", "c")
TILE = 8


def parity_of():
    return lax.axis_index("c")


def front_kernel(
    scale, groups, count_hbm, fine_ref, avg_ref, out_hbm, part_ref, buf, acc, count_ref, sems, out_sems, count_sem
):
    slots, children, cells, width = buf.shape
    half = slots // 2
    parity = parity_of()

    def load(slot):
        return pltpu.make_async_copy(fine_ref.at[slot], buf.at[slot], sems.at[slot])

    load_count = pltpu.make_async_copy(count_hbm, count_ref, count_sem.at[0])
    load_count.start()

    first_sent = half * (1 - parity)
    first_kept = half * parity

    def start(k, _, first):
        load(first + k).start()
        return 0

    for first in (first_sent, first_kept):
        lax.fori_loop(0, half, functools.partial(start, first=first), 0)
    load_count.wait()
    count = count_ref[0]
    rows = 32

    def send_out(k):
        return pltpu.make_async_copy(avg_ref.at[first_sent + k], out_hbm.at[k], out_sems.at[k])

    def averaged(slot):
        factor = jnp.where(slot < count, 1.0 / children, 0.0)
        for first in range(0, cells, rows):
            total = buf[slot, 0, first : first + rows, :].astype(jnp.float32)
            for child in range(1, children):
                total += buf[slot, child, first : first + rows, :].astype(jnp.float32)
            avg_ref[slot, first : first + rows, :] = (total * factor).astype(jnp.bfloat16)

    def body(k, _, first):
        load(first + k).wait()
        averaged(first + k)
        if first is first_sent:
            send_out(k).start()
        return 0

    def cross(slot, many):
        value = avg_ref[pl.ds(slot, many)].reshape(many * cells, width)
        return lax.dot_general(value, value, (((0,), (0,)), ((), ())), preferred_element_type=jnp.float32)

    acc[...] = jnp.zeros_like(acc)
    for first, runs in zip((first_sent, first_kept), groups):
        done = 0
        for many in runs:
            lax.fori_loop(done, done + many, functools.partial(body, first=first), 0)
            acc[...] += cross(first + done, many)
            done += many
    lane = lax.broadcasted_iota(jnp.int32, (width // 4, width), 1)
    strips = [acc[i : i + width // 4, :] * scale for i in range(0, width, width // 4)]
    second = jnp.where(lane < width // 4, pltpu.roll(strips[3], width // 4, 1), strips[1])
    cut = width // 8
    third = jnp.where(lane[:cut] < width // 2, pltpu.roll(strips[2][cut:], width // 2, 1), strips[2][:cut])
    packed = jnp.concatenate([strips[0], second, third], axis=0)
    members, cores, middle, _ = part_ref.shape
    for core in range(cores):
        for member in range(members):
            part_ref[member, core] = packed[core * middle : (core + 1) * middle]

    def finish(k, _):
        send_out(k).wait()
        return 0

    lax.fori_loop(0, half, finish, 0)


def unpacked(packed):
    width = packed.shape[1]
    quarter, cut = width // 4, width // 8
    second, third = packed[quarter : 2 * quarter], packed[2 * quarter :]
    upper = jnp.concatenate(
        [packed[: 2 * quarter], third, pltpu.roll(third, width // 2, 1), pltpu.roll(second, width - quarter, 1)], axis=0
    )
    row = lax.broadcasted_iota(jnp.int32, upper.shape, 0)
    lane = lax.broadcasted_iota(jnp.int32, upper.shape, 1)
    return jnp.where(lane // quarter >= row // quarter, upper, upper.T)


def lane_spread(tile, lane):
    return jnp.broadcast_to(tile[:, lane : lane + 1], tile.shape)


def row_spread(tile, row):
    return jnp.broadcast_to(tile[row : row + 1, :], tile.shape)


def three_terms(value):
    terms = []
    for _ in range(3):
        term = value.astype(jnp.bfloat16)
        terms.append(term)
        value = value - term.astype(jnp.float32)
    return terms


def eliminate(rows, near=3):
    shape = rows[0].shape
    lane = lax.broadcasted_iota(jnp.int32, shape, 1)
    sub = lax.broadcasted_iota(jnp.int32, shape, 0)
    zero = lane.astype(jnp.float32) * 0.0
    rows = list(rows)
    tiles = len(rows)
    factor, inverse = [], []

    def columns_of(tile, base):
        return [lane_spread(tile, base + c) + zero for c in range(TILE)]

    ahead = columns_of(rows[0], 0)
    for t in range(tiles):
        base = t * TILE
        inside = (lane >= base) & (lane < base + TILE)
        last = min(tiles, t + 1 + near)
        columns = {j: columns_of(rows[j], base) for j in range(t + 1, last)}
        after = columns_of(rows[t + 1], base + TILE) if t + 1 < tiles else None
        d = [[row_spread(ahead[c], i) for c in range(i + 1)] for i in range(TILE)]
        mixed = [
            jnp.where(inside, (lane == base + i).astype(jnp.float32), row_spread(rows[t], i)) for i in range(TILE)
        ]
        inv = [None] * TILE
        for r in range(TILE):
            inv[r] = lax.rsqrt(d[r][r])
            for i in range(r + 1, TILE):
                d[i][r] = d[i][r] * inv[r]
            mixed[r] = mixed[r] * inv[r]
            for i in range(r + 1, TILE):
                for c in range(r + 1, i + 1):
                    d[i][c] = d[i][c] - d[i][r] * d[c][r]
                mixed[i] = mixed[i] - d[i][r] * mixed[r]
        for j in range(t + 1, last):
            b = columns[j]
            rest = jnp.where(inside, 0.0, rows[j])
            for r in range(TILE):
                b[r] = b[r] * inv[r]
                for c in range(r + 1, TILE):
                    b[c] = b[c] - b[r] * d[c][r]
                rest = rest - b[r] * mixed[r]
                if j == t + 1:
                    for c in range(TILE):
                        after[c] = after[c] - b[r] * row_spread(b[r], c)
            rows[j] = rest
        ahead = after
        whole = mixed[0]
        for r in range(1, TILE):
            whole = jnp.where(sub == r, mixed[r], whole)
        past = lane >= base + TILE
        upper = jnp.where(past, whole, 0.0)
        if last < tiles:
            u, y = three_terms(upper), three_terms(whole)
            left = jnp.concatenate([u[0], u[0], u[1], u[1], u[0], u[2]], axis=0)
            right = jnp.concatenate([y[0], y[1], y[0], y[1], y[2], y[0]], axis=0)
            product = lax.dot_general(left, right, (((0,), (0,)), ((), ())), preferred_element_type=jnp.float32)
            for j in range(last, tiles):
                rows[j] = jnp.where(inside, 0.0, rows[j]) - product[j * TILE : (j + 1) * TILE]
        for c in range(TILE):
            column = d[c][c] * inv[c]
            for r in range(c):
                column = jnp.where(sub == r, d[c][r], column)
            upper = jnp.where((lane == base + c) & (sub <= c), column, upper)
        factor.append(upper)
        inverse.append(jnp.where(past, 0.0, whole))
    return factor, inverse


def back_kernel(
    count_hbm, place_hbm, mine_ref, other_ref, own_ref, moved_ref, factor_ref, modes_ref, gram, inv, buf, out, count_ref, place_ref, in_sems, out_sems
):
    blocks, cells, width = out.shape
    slots = buf.shape[0] - blocks
    parity = parity_of()
    loads = (
        pltpu.make_async_copy(count_hbm, count_ref, in_sems.at[2]),
        pltpu.make_async_copy(place_hbm, place_ref, in_sems.at[3]),
        pltpu.make_async_copy(own_ref, buf.at[pl.ds(0, slots)], in_sems.at[0]),
        pltpu.make_async_copy(moved_ref, buf.at[pl.ds(slots, blocks)], in_sems.at[1]),
    )
    for load in loads:
        load.start()
    mine, other = mine_ref[...], other_ref[...]
    packed = jnp.concatenate([jnp.where(parity == 0, mine, other), jnp.where(parity == 0, other, mine)], axis=0)
    gram[...] = unpacked(packed)
    factor, inverse = eliminate([gram[i : i + TILE, :] for i in range(0, width, TILE)])
    for t in range(width // TILE):
        factor_ref[t * TILE : (t + 1) * TILE, :] = factor[t]
        inv[t * TILE : (t + 1) * TILE, :] = inverse[t]
    for load in loads:
        load.wait()
    count = count_ref[0]
    parts = three_terms(inv[...])
    terms = jnp.concatenate(
        [jnp.concatenate(parts[:2], axis=1), jnp.concatenate([parts[2], jnp.zeros_like(parts[2])], axis=1)], axis=0
    )

    def store(i):
        return pltpu.make_async_copy(out.at[i], modes_ref.at[pl.ds(i * cells, cells)], out_sems.at[i])

    for i in range(blocks):
        wanted = place_ref[0, i]
        excess = blocks - count
        from_even = jnp.where(wanted < count, wanted, slots + wanted - count)
        from_odd = jnp.where(wanted < excess, slots + wanted, wanted - excess)
        index = jnp.where(parity == 0, from_even, from_odd)
        value = buf[index]
        repeated = jnp.concatenate([value, value], axis=1)
        both = lax.dot_general(repeated, terms, (((1,), (1,)), ((), ())), preferred_element_type=jnp.float32)
        total = both[:, :width] + both[:, width:]
        out[i] = total.astype(jnp.bfloat16)
        store(i).start()
    for i in range(blocks):
        store(i).wait()


def swapped(value):
    return lax.ppermute(value, "c", [(0, 1), (1, 0)])


def groups_of(total):
    return [total], [total // 2, total // 2 - 2, 2]


def shards(fine, patch_count, block_place):
    slots, children, cells, width = fine.shape
    blocks = slots // 2
    devices = 1
    for axis in ALL:
        devices *= lax.axis_size(axis)
    row_total = blocks * cells * devices
    vmem, hbm = pltpu.VMEM, pl.ANY
    spec = lambda space: pl.BlockSpec(memory_space=space)
    own, outgoing, parts = pl.pallas_call(
        functools.partial(front_kernel, 1.0 / row_total, groups_of(blocks)),
        out_shape=(
            jax.ShapeDtypeStruct((slots, cells, width), jnp.bfloat16),
            jax.ShapeDtypeStruct((blocks, cells, width), jnp.bfloat16),
            jax.ShapeDtypeStruct((lax.axis_size("z"), 2, width * 5 // 16, width), jnp.float32),
        ),
        in_specs=[spec(hbm), spec(hbm)],
        out_specs=[spec(vmem), spec(pltpu.HBM), spec(vmem)],
        scratch_shapes=[
            pltpu.VMEM(fine.shape, jnp.bfloat16),
            pltpu.VMEM((width, width), jnp.float32),
            pltpu.SMEM((1,), jnp.int32),
            pltpu.SemaphoreType.DMA((slots,)),
            pltpu.SemaphoreType.DMA((blocks,)),
            pltpu.SemaphoreType.DMA((1,)),
        ],
        compiler_params=pltpu.CompilerParams(vmem_limit_bytes=50 * 2**20),
        name="front",
    )(patch_count, fine)
    parts = parts.reshape((-1,) + parts.shape[2:])
    half = jnp.sum(lax.all_to_all(parts, ("z", "c"), 0, 0), axis=0)

    moved = swapped(outgoing)
    sent = jnp.broadcast_to(half[None], (lax.axis_size("x") * lax.axis_size("y"),) + half.shape)
    half = jnp.sum(lax.all_to_all(sent, ("x", "y"), 0, 0), axis=0)
    other = swapped(half)
    factor, modes = pl.pallas_call(
        back_kernel,
        out_shape=(
            jax.ShapeDtypeStruct((width, width), jnp.float32),
            jax.ShapeDtypeStruct((blocks * cells, width), jnp.bfloat16),
        ),
        in_specs=[spec(hbm), spec(hbm), spec(vmem), spec(vmem), spec(hbm), spec(hbm)],
        out_specs=[spec(vmem), spec(hbm)],
        scratch_shapes=[
            pltpu.VMEM((width, width), jnp.float32),
            pltpu.VMEM((width, width), jnp.float32),
            pltpu.VMEM((slots + blocks, cells, width), jnp.bfloat16),
            pltpu.VMEM((blocks, cells, width), jnp.bfloat16),
            pltpu.SMEM((1,), jnp.int32),
            pltpu.SMEM((1, blocks), jnp.int32),
            pltpu.SemaphoreType.DMA((4,)),
            pltpu.SemaphoreType.DMA((blocks,)),
        ],
        compiler_params=pltpu.CompilerParams(vmem_limit_bytes=20 * 2**20),
        name="back",
    )(patch_count, block_place, half, other, own, moved)
    return (factor, modes)


def solution(mesh):
    sizes = mesh.shape
    finer = Mesh(mesh.devices.reshape(4, sizes["gx"] // 4, sizes["gy"] // 2, 2), ALL)
    return jax.shard_map(
        shards,
        mesh=finer,
        in_specs=(P(ALL, None, None, None), P(ALL), P(ALL, None)),
        out_specs=(P(), P(ALL, None)),
        check_vma=False,
    )
```

```python
import functools

import jax
import jax.numpy as jnp
from jax import lax
from jax.experimental import pallas as pl
from jax.experimental.pallas import tpu as pltpu
from jax.sharding import Mesh
from jax.sharding import PartitionSpec as P

ALL = ("x", "y", "z", "c")
TILE = 8


def parity_of():
    return lax.axis_index("c")


def front_kernel(
    scale, groups, count_hbm, fine_ref, avg_ref, out_hbm, part_ref, buf, acc, count_ref, sems, out_sems, count_sem
):
    slots, children, cells, width = buf.shape
    half = slots // 2
    parity = parity_of()

    def load(slot):
        return pltpu.make_async_copy(fine_ref.at[slot], buf.at[slot], sems.at[slot])

    load_count = pltpu.make_async_copy(count_hbm, count_ref, count_sem.at[0])
    load_count.start()

    first_sent = half * (1 - parity)
    first_kept = half * parity

    def start(k, _, first):
        load(first + k).start()
        return 0

    for first in (first_sent, first_kept):
        lax.fori_loop(0, half, functools.partial(start, first=first), 0)
    load_count.wait()
    count = count_ref[0]
    rows = 32

    def send_out(k):
        return pltpu.make_async_copy(avg_ref.at[first_sent + k], out_hbm.at[k], out_sems.at[k])

    def averaged(slot):
        factor = jnp.where(slot < count, 1.0 / children, 0.0)
        for first in range(0, cells, rows):
            total = buf[slot, 0, first : first + rows, :].astype(jnp.float32)
            for child in range(1, children):
                total += buf[slot, child, first : first + rows, :].astype(jnp.float32)
            avg_ref[slot, first : first + rows, :] = (total * factor).astype(jnp.bfloat16)

    def body(k, _, first):
        load(first + k).wait()
        averaged(first + k)
        if first is first_sent:
            send_out(k).start()
        return 0

    def cross(slot, many):
        value = avg_ref[pl.ds(slot, many)].reshape(many * cells, width)
        return lax.dot_general(value, value, (((0,), (0,)), ((), ())), preferred_element_type=jnp.float32)

    acc[...] = jnp.zeros_like(acc)
    for first, runs in zip((first_sent, first_kept), groups):
        done = 0
        for many in runs:
            lax.fori_loop(done, done + many, functools.partial(body, first=first), 0)
            acc[...] += cross(first + done, many)
            done += many
    lane = lax.broadcasted_iota(jnp.int32, (width // 4, width), 1)
    strips = [acc[i : i + width // 4, :] * scale for i in range(0, width, width // 4)]
    second = jnp.where(lane < width // 4, pltpu.roll(strips[3], width // 4, 1), strips[1])
    cut = width // 8
    third = jnp.where(lane[:cut] < width // 2, pltpu.roll(strips[2][cut:], width // 2, 1), strips[2][:cut])
    packed = jnp.concatenate([strips[0], second, third], axis=0)
    members, cores, middle, _ = part_ref.shape
    for core in range(cores):
        for member in range(members):
            part_ref[member, core] = packed[core * middle : (core + 1) * middle]

    def finish(k, _):
        send_out(k).wait()
        return 0

    lax.fori_loop(0, half, finish, 0)


def unpacked(packed):
    width = packed.shape[1]
    quarter, cut = width // 4, width // 8
    second, third = packed[quarter : 2 * quarter], packed[2 * quarter :]
    upper = jnp.concatenate(
        [packed[: 2 * quarter], third, pltpu.roll(third, width // 2, 1), pltpu.roll(second, width - quarter, 1)], axis=0
    )
    row = lax.broadcasted_iota(jnp.int32, upper.shape, 0)
    lane = lax.broadcasted_iota(jnp.int32, upper.shape, 1)
    return jnp.where(lane // quarter >= row // quarter, upper, upper.T)


def lane_spread(tile, lane):
    return jnp.broadcast_to(tile[:, lane : lane + 1], tile.shape)


def row_spread(tile, row):
    return jnp.broadcast_to(tile[row : row + 1, :], tile.shape)


def three_terms(value):
    terms = []
    for _ in range(3):
        term = value.astype(jnp.bfloat16)
        terms.append(term)
        value = value - term.astype(jnp.float32)
    return terms


def eliminate(rows, near=3):
    shape = rows[0].shape
    lane = lax.broadcasted_iota(jnp.int32, shape, 1)
    sub = lax.broadcasted_iota(jnp.int32, shape, 0)
    zero = lane.astype(jnp.float32) * 0.0
    rows = list(rows)
    tiles = len(rows)
    factor, inverse = [], []

    def columns_of(tile, base):
        return [lane_spread(tile, base + c) for c in range(TILE)]

    ahead = [column + zero for column in columns_of(rows[0], 0)]
    for t in range(tiles):
        base = t * TILE
        inside = (lane >= base) & (lane < base + TILE)
        last = min(tiles, t + 1 + near)
        columns = {j: columns_of(rows[j], base) for j in range(t + 1, last)}
        after = columns_of(rows[t + 1], base + TILE) if t + 1 < tiles else None
        d = [[row_spread(ahead[c], i) for c in range(i + 1)] for i in range(TILE)]
        mixed = [
            jnp.where(inside, (lane == base + i).astype(jnp.float32), row_spread(rows[t], i)) for i in range(TILE)
        ]
        inv = [None] * TILE
        for r in range(TILE):
            inv[r] = lax.rsqrt(d[r][r])
            for i in range(r + 1, TILE):
                d[i][r] = d[i][r] * inv[r]
            mixed[r] = mixed[r] * inv[r]
            for i in range(r + 1, TILE):
                for c in range(r + 1, i + 1):
                    d[i][c] = d[i][c] - d[i][r] * d[c][r]
                mixed[i] = mixed[i] - d[i][r] * mixed[r]
        for j in range(t + 1, last):
            b = columns[j]
            rest = jnp.where(inside, 0.0, rows[j])
            for r in range(TILE):
                b[r] = b[r] * inv[r]
                for c in range(r + 1, TILE):
                    b[c] = b[c] - b[r] * d[c][r]
                rest = rest - b[r] * mixed[r]
                if j == t + 1:
                    for c in range(TILE):
                        after[c] = after[c] - b[r] * row_spread(b[r], c)
            rows[j] = rest
        ahead = after
        whole = mixed[0]
        for r in range(1, TILE):
            whole = jnp.where(sub == r, mixed[r], whole)
        past = lane >= base + TILE
        upper = jnp.where(past, whole, 0.0)
        if last < tiles:
            u, y = three_terms(upper), three_terms(whole)
            left = jnp.concatenate([u[0], u[0], u[1], u[1], u[0], u[2]], axis=0)
            right = jnp.concatenate([y[0], y[1], y[0], y[1], y[2], y[0]], axis=0)
            product = lax.dot_general(left, right, (((0,), (0,)), ((), ())), preferred_element_type=jnp.float32)
            for j in range(last, tiles):
                rows[j] = jnp.where(inside, 0.0, rows[j]) - product[j * TILE : (j + 1) * TILE]
        for c in range(TILE):
            column = d[c][c] * inv[c]
            for r in range(c):
                column = jnp.where(sub == r, d[c][r], column)
            upper = jnp.where((lane == base + c) & (sub <= c), column, upper)
        factor.append(upper)
        inverse.append(jnp.where(past, 0.0, whole))
    return factor, inverse


def back_kernel(
    count_hbm, place_hbm, mine_ref, other_ref, own_ref, moved_ref, factor_ref, modes_ref, gram, inv, buf, out, count_ref, place_ref, in_sems, out_sems
):
    blocks, cells, width = out.shape
    slots = buf.shape[0] - blocks
    parity = parity_of()
    loads = (
        pltpu.make_async_copy(count_hbm, count_ref, in_sems.at[2]),
        pltpu.make_async_copy(place_hbm, place_ref, in_sems.at[3]),
        pltpu.make_async_copy(own_ref, buf.at[pl.ds(0, slots)], in_sems.at[0]),
        pltpu.make_async_copy(moved_ref, buf.at[pl.ds(slots, blocks)], in_sems.at[1]),
    )
    for load in loads:
        load.start()
    mine, other = mine_ref[...], other_ref[...]
    packed = jnp.concatenate([jnp.where(parity == 0, mine, other), jnp.where(parity == 0, other, mine)], axis=0)
    gram[...] = unpacked(packed)
    factor, inverse = eliminate([gram[i : i + TILE, :] for i in range(0, width, TILE)])
    for t in range(width // TILE):
        factor_ref[t * TILE : (t + 1) * TILE, :] = factor[t]
        inv[t * TILE : (t + 1) * TILE, :] = inverse[t]
    for load in loads:
        load.wait()
    count = count_ref[0]
    parts = three_terms(inv[...])
    terms = jnp.concatenate(
        [jnp.concatenate(parts[:2], axis=1), jnp.concatenate([parts[2], jnp.zeros_like(parts[2])], axis=1)], axis=0
    )

    def store(i):
        return pltpu.make_async_copy(out.at[i], modes_ref.at[pl.ds(i * cells, cells)], out_sems.at[i])

    for i in range(blocks):
        wanted = place_ref[0, i]
        excess = blocks - count
        from_even = jnp.where(wanted < count, wanted, slots + wanted - count)
        from_odd = jnp.where(wanted < excess, slots + wanted, wanted - excess)
        index = jnp.where(parity == 0, from_even, from_odd)
        value = buf[index]
        repeated = jnp.concatenate([value, value], axis=1)
        both = lax.dot_general(repeated, terms, (((1,), (1,)), ((), ())), preferred_element_type=jnp.float32)
        total = both[:, :width] + both[:, width:]
        out[i] = total.astype(jnp.bfloat16)
        store(i).start()
    for i in range(blocks):
        store(i).wait()


def swapped(value):
    return lax.ppermute(value, "c", [(0, 1), (1, 0)])


def groups_of(total):
    return [total], [total // 2, total // 2 - 2, 2]


def shards(fine, patch_count, block_place):
    slots, children, cells, width = fine.shape
    blocks = slots // 2
    devices = 1
    for axis in ALL:
        devices *= lax.axis_size(axis)
    row_total = blocks * cells * devices
    vmem, hbm = pltpu.VMEM, pl.ANY
    spec = lambda space: pl.BlockSpec(memory_space=space)
    own, outgoing, parts = pl.pallas_call(
        functools.partial(front_kernel, 1.0 / row_total, groups_of(blocks)),
        out_shape=(
            jax.ShapeDtypeStruct((slots, cells, width), jnp.bfloat16),
            jax.ShapeDtypeStruct((blocks, cells, width), jnp.bfloat16),
            jax.ShapeDtypeStruct((lax.axis_size("z"), 2, width * 5 // 16, width), jnp.float32),
        ),
        in_specs=[spec(hbm), spec(hbm)],
        out_specs=[spec(vmem), spec(pltpu.HBM), spec(vmem)],
        scratch_shapes=[
            pltpu.VMEM(fine.shape, jnp.bfloat16),
            pltpu.VMEM((width, width), jnp.float32),
            pltpu.SMEM((1,), jnp.int32),
            pltpu.SemaphoreType.DMA((slots,)),
            pltpu.SemaphoreType.DMA((blocks,)),
            pltpu.SemaphoreType.DMA((1,)),
        ],
        compiler_params=pltpu.CompilerParams(vmem_limit_bytes=50 * 2**20),
        name="front",
    )(patch_count, fine)
    parts = parts.reshape((-1,) + parts.shape[2:])
    half = jnp.sum(lax.all_to_all(parts, ("z", "c"), 0, 0), axis=0)

    moved = swapped(outgoing)
    sent = jnp.broadcast_to(half[None], (lax.axis_size("x") * lax.axis_size("y"),) + half.shape)
    half = jnp.sum(lax.all_to_all(sent, ("x", "y"), 0, 0), axis=0)
    other = swapped(half)
    factor, modes = pl.pallas_call(
        back_kernel,
        out_shape=(
            jax.ShapeDtypeStruct((width, width), jnp.float32),
            jax.ShapeDtypeStruct((blocks * cells, width), jnp.bfloat16),
        ),
        in_specs=[spec(hbm), spec(hbm), spec(vmem), spec(vmem), spec(hbm), spec(hbm)],
        out_specs=[spec(vmem), spec(hbm)],
        scratch_shapes=[
            pltpu.VMEM((width, width), jnp.float32),
            pltpu.VMEM((width, width), jnp.float32),
            pltpu.VMEM((slots + blocks, cells, width), jnp.bfloat16),
            pltpu.VMEM((blocks, cells, width), jnp.bfloat16),
            pltpu.SMEM((1,), jnp.int32),
            pltpu.SMEM((1, blocks), jnp.int32),
            pltpu.SemaphoreType.DMA((4,)),
            pltpu.SemaphoreType.DMA((blocks,)),
        ],
        compiler_params=pltpu.CompilerParams(vmem_limit_bytes=20 * 2**20),
        name="back",
    )(patch_count, block_place, half, other, own, moved)
    return (factor, modes)


def solution(mesh):
    sizes = mesh.shape
    finer = Mesh(mesh.devices.reshape(4, sizes["gx"] // 4, sizes["gy"] // 2, 2), ALL)
    return jax.shard_map(
        shards,
        mesh=finer,
        in_specs=(P(ALL, None, None, None), P(ALL), P(ALL, None)),
        out_specs=(P(), P(ALL, None)),
        check_vma=False,
    )
```
